256 devices in a mesh: section: 16 (over z, core), mon: 16 (over x, y).
Axes of the slice: x: 4, y: 4, z: 8, core: 2. Of those that a mesh axis runs over, the one named last changes fastest.
Arguments:
- stream_one: float32 [8192, 128], P('mon'), may hold values from -6 to 6
- stream_two: float32 [8192, 128], P('mon'), may hold values from -6 to 6
- cotan_one: float32 [8192, 128], P('mon'), may hold values from -6 to 6
- cotan_two: float32 [8192, 128], P('mon'), may hold values from -6 to 6
- first_up: bfloat16 [16, 128, 64, 256], P('section', 'mon'), may hold values from -0.75 to 0.75
- first_down: bfloat16 [16, 128, 256, 64], P('section', 'mon'), may hold values from -0.09375 to 0.09375
- second_up: bfloat16 [16, 128, 64, 256], P('section', 'mon'), may hold values from -0.75 to 0.75
- second_down: bfloat16 [16, 128, 256, 64], P('section', 'mon'), may hold values from -0.09375 to 0.09375
Outputs:
- grad_first_up: float32 [16, 128, 64, 256], P('section', 'mon')
- grad_first_down: float32 [16, 128, 256, 64], P('section', 'mon')
- grad_second_up: float32 [16, 128, 64, 256], P('section', 'mon')
- grad_second_down: float32 [16, 128, 256, 64], P('section', 'mon')
The draws below stay inside these ranges and needn't reach their ends.
All inputs are finite; a program needn't handle non-finite values.
Results may differ from the reference program's by a relative error of at most 0.014.
Values may be sent and summed in bfloat16 or wider, within the bound.
A program may use at most 64 MiB of HBM per device.

```python
import math
import jax
import jax.numpy as jnp

BLOCKS = 128
BIN = 64
UNITS = 256
D = 8192
PAIR = 2
LAYERS = 16
TOKENS = 128


def steps_of(stream_key, extent, shards, least, top_value):
    level, own = 1.0, jax.random.fold_in(stream_key, 6)
    for axis_at, blocks in shards:
        steps = jnp.exp(jax.random.uniform(jax.random.fold_in(own, axis_at), (blocks,), jnp.float32, least / len(shards), top_value / len(shards)))
        level = level * jnp.repeat(steps, extent[axis_at] // blocks).reshape([-1 if axis == axis_at else 1 for axis in range(len(extent))])
    return level


def scatter_about(own_key, extent, spread, limit, shards=(), held_as=jnp.bfloat16):
    array = jax.random.normal(own_key, extent, jnp.float32) * spread
    if len(shards) > 0:
        array = steps_of(own_key, extent, shards, -0.22, 0.18) * array
    return jnp.clip(array, min=-limit, max=limit).astype(held_as)


def setup_inputs(seed: int = 0) -> dict:
    key_list = jax.random.split(jax.random.key(seed), 9)
    return {
        "stream_one": scatter_about(key_list[0], (D, TOKENS), 1.0, 6.0, ((0, 16),), jnp.float32),
        "stream_two": scatter_about(key_list[1], (D, TOKENS), 1.0, 6.0, ((0, 16),), jnp.float32),
        "cotan_one": scatter_about(key_list[2], (D, TOKENS), 1.0, 6.0, ((0, 16),), jnp.float32),
        "cotan_two": scatter_about(key_list[3], (D, TOKENS), 1.0, 6.0, ((0, 16),), jnp.float32),
        "first_up": scatter_about(key_list[4], (LAYERS, BLOCKS, BIN, UNITS), BIN ** -0.5, 0.75, ((0, 16), (1, 16))),
        "first_down": scatter_about(key_list[5], (LAYERS, BLOCKS, UNITS, BIN), (16 * UNITS) ** -0.5, 0.09375, ((0, 16), (1, 16))),
        "second_up": scatter_about(key_list[6], (LAYERS, BLOCKS, BIN, UNITS), BIN ** -0.5, 0.75, ((0, 16), (1, 16))),
        "second_down": scatter_about(key_list[7], (LAYERS, BLOCKS, UNITS, BIN), (16 * UNITS) ** -0.5, 0.09375, ((0, 16), (1, 16))),
    }


def monarch_forward(stream, w_up, w_down):
    tokens = stream.shape[1]
    feed = stream.astype(jnp.bfloat16).reshape(BLOCKS, BIN, tokens)
    pre_act = jnp.einsum('bit,bio->bot', feed.astype(jnp.float32), w_up.astype(jnp.float32))
    hidden = jax.nn.silu(pre_act).astype(jnp.bfloat16)
    grouped = hidden.reshape(BLOCKS, BLOCKS, PAIR, tokens).transpose(1, 2, 0, 3).reshape(BLOCKS, UNITS, tokens)
    output = jnp.einsum('gjt,gjo->got', grouped.astype(jnp.float32), w_down.astype(jnp.float32))
    return (feed, pre_act, grouped, output.reshape(D, tokens))

def monarch_backward(cotangent, feed, pre_act, grouped, w_up, w_down):
    tokens = cotangent.shape[1]
    cot_bf = cotangent.astype(jnp.bfloat16).reshape(BLOCKS, BIN, tokens)
    grad_down = jnp.einsum('gjt,got->gjo', grouped.astype(jnp.float32), cot_bf.astype(jnp.float32))
    back = jnp.einsum('got,gjo->gjt', cot_bf.astype(jnp.float32), w_down.astype(jnp.float32)).astype(jnp.bfloat16)
    d_hidden = back.reshape(BLOCKS, PAIR, BLOCKS, tokens).transpose(2, 0, 1, 3).reshape(BLOCKS, UNITS, tokens)
    sig = jax.nn.sigmoid(pre_act)
    slope = sig * (1.0 + pre_act * (1.0 - sig))
    d_pre = (d_hidden.astype(jnp.float32) * slope).astype(jnp.bfloat16)
    grad_up = jnp.einsum('bit,bot->bio', feed.astype(jnp.float32), d_pre.astype(jnp.float32))
    d_in = jnp.einsum('bot,bio->bit', d_pre.astype(jnp.float32), w_up.astype(jnp.float32))
    return (grad_up, grad_down, d_in.reshape(D, tokens))

def reference(stream_one, stream_two, cotan_one, cotan_two, first_up, first_down, second_up, second_down):
    scale = 1.0 / math.sqrt(TOKENS)
    upper_one, upper_two = (stream_one, stream_two)
    carry_one, carry_two = (cotan_one, cotan_two)
    store_fu, store_fd, store_gu, store_gd = ([], [], [], [])
    for layer in range(LAYERS - 1, -1, -1):
        feed_g, pre_g, grouped_g, out_g = monarch_forward(upper_one, second_up[layer], second_down[layer])
        lower_two = upper_two - out_g
        gu_term, gd_term, back_g = monarch_backward(carry_two, feed_g, pre_g, grouped_g, second_up[layer], second_down[layer])
        total_one = carry_one + back_g
        feed_f, pre_f, grouped_f, out_f = monarch_forward(lower_two, first_up[layer], first_down[layer])
        lower_one = upper_one - out_f
        fu_term, fd_term, back_f = monarch_backward(total_one, feed_f, pre_f, grouped_f, first_up[layer], first_down[layer])
        total_two = carry_two + back_f
        store_fu.append(fu_term * scale)
        store_fd.append(fd_term * scale)
        store_gu.append(gu_term * scale)
        store_gd.append(gd_term * scale)
        upper_one, upper_two = (lower_one, lower_two)
        carry_one, carry_two = (total_one, total_two)
    return (jnp.stack(store_fu[::-1]), jnp.stack(store_fd[::-1]), jnp.stack(store_gu[::-1]), jnp.stack(store_gd[::-1]))
```

```python
import functools
import math

import jax
import jax.numpy as jnp
from jax import lax
from jax.experimental import pallas as pl
from jax.experimental.pallas import tpu as pltpu
from jax.sharding import PartitionSpec as P

MESH = pl.DeviceIdType.MESH
F32, BF16 = jnp.float32, jnp.bfloat16

ITEMS = 8
TOK = 8
FEAT = 64
LANES = 128
ROWS = ITEMS * TOK


def chain_kernel(
    sections, mons, scale,
    w_hbm, one_in, two_in, cone_in, ctwo_in, grad_ref,
    wbuf, one, two, cone, ctwo, slope, masked_g, masked_d, send, recv, bun, xc, gbun, gxc, items,
    wsem, send_sem, recv_sem, bun_sem, xc_sem, gbun_sem, gxc_sem,
):
    sec = lax.axis_index("section")
    me = lax.axis_index("mon")
    width = mons * LANES
    chunk = 2 * LANES
    chunks = width // chunk

    barrier = pltpu.get_barrier_semaphore()
    for k in range(1, mons):
        pl.semaphore_signal(barrier, inc=1, device_id={"mon": (me + k) % mons}, device_id_type=MESH)
    for k in range(1, sections):
        pl.semaphore_signal(barrier, inc=1, device_id={"section": (sec + k) % sections}, device_id_type=MESH)

    def fetch(layer, slot):
        return pltpu.make_async_copy(w_hbm.at[layer], wbuf.at[slot], wsem.at[slot])

    fetch(sections - 1, 0).start()
    one[...] = one_in[...]
    two[...] = two_in[...]
    cone[...] = cone_in[...]
    ctwo[...] = ctwo_in[...]
    pl.semaphore_wait(barrier, mons + sections - 2)

    lane = lax.broadcasted_iota(jnp.int32, (TOK, chunk), 1) % LANES
    of_block = lane // 16
    of_group = (lane // 2) % 8

    def diagonal(full, which):
        picked = full[0:TOK]
        for k in range(1, ITEMS):
            picked = jnp.where(which == k, full[k * TOK:(k + 1) * TOK], picked)
        return picked

    def spread(values, which):
        return jnp.concatenate(
            [jnp.where(which == k, values, 0.0) for k in range(ITEMS)], axis=0
        ).astype(BF16)

    def half_step(step, half, wslot, w_up, w_down, source, target, cot, carry):
        layer = sections - 1 - step
        feed = source[...].astype(BF16)
        cot_bf = cot[...].astype(BF16)

        @pl.when(step > 0)
        def _():
            pltpu.make_async_copy(send.at[half, pl.ds(0, mons - 1)], send.at[half, pl.ds(0, mons - 1)], send_sem.at[half]).wait()
            pltpu.make_async_copy(bun.at[half], bun.at[half], bun_sem.at[half]).wait()
            pltpu.make_async_copy(xc.at[half], xc.at[half], xc_sem.at[half]).wait()

        for n in range(chunks):
            cols = pl.ds(n * chunk, chunk)
            pre = diagonal(jnp.dot(feed, wbuf[wslot, w_up, :, cols], preferred_element_type=F32), of_block)
            back = diagonal(jnp.dot(cot_bf, wbuf[wslot, w_down, :, cols], preferred_element_type=F32), of_group)
            sig = 1.0 / (1.0 + jnp.exp(-pre))
            slope[:, cols] = sig * (1.0 + pre * (1.0 - sig))
            tile = jnp.concatenate([pre * sig, back], axis=0).astype(BF16)
            send[half, 2 * n] = tile[:, 0:LANES]
            send[half, 2 * n + 1] = tile[:, LANES:chunk]

        for k in range(1, mons):
            peer = (me + k) % mons
            pltpu.make_async_remote_copy(
                src_ref=send.at[half, peer], dst_ref=recv.at[half, me],
                send_sem=send_sem.at[half], recv_sem=recv_sem.at[half],
                device_id={"mon": peer}, device_id_type=MESH,
            ).start()
        recv[half, me] = send[half, me]
        xc[half, :, 0:FEAT] = feed
        xc[half, :, FEAT:LANES] = cot_bf
        pltpu.make_async_copy(recv.at[half, pl.ds(0, mons - 1)], recv.at[half, pl.ds(0, mons - 1)], recv_sem.at[half]).wait()

        for n in range(chunks):
            cols = pl.ds(n * chunk, chunk)
            arrived = jnp.concatenate([recv[half, 2 * n], recv[half, 2 * n + 1]], axis=1).astype(F32)
            grouped = arrived[0:TOK]
            dpre = arrived[TOK:2 * TOK] * slope[:, cols]
            masked_g[:, cols] = spread(grouped, of_group)
            masked_d[:, cols] = spread(dpre, of_block)
            bun[half, :, cols] = jnp.concatenate([grouped, dpre], axis=0).astype(BF16)
        trans = (((1,), (1,)), ((), ()))
        target[...] -= lax.dot_general(masked_g[...], wbuf[wslot, w_down], trans, preferred_element_type=F32)
        carry[...] += lax.dot_general(masked_d[...], wbuf[wslot, w_up], trans, preferred_element_type=F32)

        @pl.when(sec == layer)
        def _():
            pltpu.make_async_copy(bun.at[half], gbun.at[half, sec], bun_sem.at[half]).start()
            pltpu.make_async_copy(xc.at[half], gxc.at[half, sec], xc_sem.at[half]).start()

        @pl.when(sec != layer)
        def _():
            pltpu.make_async_remote_copy(
                src_ref=bun.at[half], dst_ref=gbun.at[half, sec],
                send_sem=bun_sem.at[half], recv_sem=gbun_sem.at[half],
                device_id={"section": layer}, device_id_type=MESH,
            ).start()
            pltpu.make_async_remote_copy(
                src_ref=xc.at[half], dst_ref=gxc.at[half, sec],
                send_sem=xc_sem.at[half], recv_sem=gxc_sem.at[half],
                device_id={"section": layer}, device_id_type=MESH,
            ).start()

    def layer_step(step, carry):
        wslot = step % 2
        fetch(0, wslot).wait()

        @pl.when(step + 1 < sections)
        def _():
            fetch(sections - 2 - step, 1 - wslot).start()

        half_step(step, 0, wslot, 2, 3, one, two, ctwo, cone)
        half_step(step, 1, wslot, 0, 1, two, one, cone, ctwo)
        return carry

    lax.fori_loop(0, sections, layer_step, 0)

    for half in range(2):
        pltpu.make_async_copy(send.at[half, pl.ds(0, mons - 1)], send.at[half, pl.ds(0, mons - 1)], send_sem.at[half]).wait()
        pltpu.make_async_copy(bun.at[half], bun.at[half], bun_sem.at[half]).wait()
        pltpu.make_async_copy(xc.at[half], xc.at[half], xc_sem.at[half]).wait()
        if sections > 1:
            part = pl.ds(0, sections - 1)
            pltpu.make_async_copy(gbun.at[half, part], gbun.at[half, part], gbun_sem.at[half]).wait()
            pltpu.make_async_copy(gxc.at[half, part], gxc.at[half, part], gxc_sem.at[half]).wait()

    left = lax.broadcasted_iota(jnp.int32, (TOK, LANES), 1) < FEAT
    row = lax.broadcasted_iota(jnp.int32, (LANES, chunk), 0)
    lane2 = lax.broadcasted_iota(jnp.int32, (LANES, chunk), 1) % LANES
    which = jnp.where(row < FEAT, lane2 // 16, (lane2 // 2) % 8)
    depth = sections * 2 * TOK
    for half in range(2):
        for s in range(sections):
            block = gxc[half, s].astype(F32)
            for k in range(ITEMS):
                piece = block[k * TOK:(k + 1) * TOK]
                items[k, s * 16:s * 16 + TOK, :] = jnp.where(left, 0.0, piece)
                items[k, s * 16 + TOK:s * 16 + 16, :] = jnp.where(left, piece, 0.0)

        def grad_chunk(n, carry):
            cols = pl.ds(pl.multiple_of(n * chunk, chunk), chunk)
            rhs = gbun[half, :, :, cols].reshape(depth, chunk)
            total = None
            for k in range(ITEMS):
                one_item = lax.dot_general(
                    items[k].astype(BF16), rhs, (((0,), (0,)), ((), ())), preferred_element_type=F32
                )
                total = one_item if total is None else jnp.where(which == k, one_item, total)
            grad_ref[half, :, cols] = total * scale
            return carry

        lax.fori_loop(0, chunks, grad_chunk, 0)


def tile_up(w):
    mons = w.shape[2] // 16
    return w.reshape(ITEMS, FEAT, mons, 16).transpose(1, 2, 0, 3).reshape(FEAT, mons * LANES)


def tile_down(w):
    mons = w.shape[1] // 16
    return w.reshape(ITEMS, 2, mons, 8, FEAT).transpose(4, 2, 3, 0, 1).reshape(FEAT, mons * LANES)


def per_device(
    stream_one, stream_two, cotan_one, cotan_two, first_up, first_down, second_up, second_down
):
    sections = lax.axis_size("section")
    mons = lax.axis_size("mon")
    sec = lax.axis_index("section")
    width = mons * LANES
    tokens = stream_one.shape[1]
    w_own = jnp.stack(
        [tile_up(first_up[0]), tile_down(first_down[0]), tile_up(second_up[0]), tile_down(second_down[0])]
    )
    w_all = lax.all_gather(w_own, "section", axis=0)

    def mine(x):
        part = lax.dynamic_slice_in_dim(x, sec * TOK, TOK, 1)
        return part.reshape(ITEMS, FEAT, TOK).transpose(0, 2, 1).reshape(ROWS, FEAT)

    vmem = pl.BlockSpec(memory_space=pltpu.VMEM)
    grads = pl.pallas_call(
        functools.partial(chain_kernel, sections, mons, 1.0 / math.sqrt(tokens)),
        out_shape=jax.ShapeDtypeStruct((2, LANES, width), F32),
        in_specs=[pl.BlockSpec(memory_space=pl.ANY), vmem, vmem, vmem, vmem],
        out_specs=vmem,
        scratch_shapes=[
            pltpu.VMEM((2, 4, FEAT, width), BF16),
            pltpu.VMEM((ROWS, FEAT), F32),
            pltpu.VMEM((ROWS, FEAT), F32),
            pltpu.VMEM((ROWS, FEAT), F32),
            pltpu.VMEM((ROWS, FEAT), F32),
            pltpu.VMEM((TOK, width), F32),
            pltpu.VMEM((ROWS, width), BF16),
            pltpu.VMEM((ROWS, width), BF16),
            pltpu.VMEM((2, mons, 2 * TOK, LANES), BF16),
            pltpu.VMEM((2, mons, 2 * TOK, LANES), BF16),
            pltpu.VMEM((2, 2 * TOK, width), BF16),
            pltpu.VMEM((2, ROWS, LANES), BF16),
            pltpu.VMEM((2, sections, 2 * TOK, width), BF16),
            pltpu.VMEM((2, sections, ROWS, LANES), BF16),
            pltpu.VMEM((ITEMS, sections * 2 * TOK, LANES), F32),
            pltpu.SemaphoreType.DMA((2,)),
            pltpu.SemaphoreType.DMA((2,)),
            pltpu.SemaphoreType.DMA((2,)),
            pltpu.SemaphoreType.DMA((2,)),
            pltpu.SemaphoreType.DMA((2,)),
            pltpu.SemaphoreType.DMA((2,)),
            pltpu.SemaphoreType.DMA((2,)),
        ],
        compiler_params=pltpu.CompilerParams(
            collective_id=0, has_side_effects=True, vmem_limit_bytes=50 * 1024 * 1024
        ),
    )(w_all, mine(stream_one), mine(stream_two), mine(cotan_one), mine(cotan_two))

    def up_grad(tiles):
        return tiles.reshape(FEAT, mons, ITEMS, 16).transpose(2, 0, 1, 3).reshape(1, ITEMS, FEAT, mons * 16)

    def down_grad(tiles):
        return tiles.reshape(FEAT, mons, 8, ITEMS, 2).transpose(3, 4, 1, 2, 0).reshape(1, ITEMS, mons * 16, FEAT)

    second, first = grads[0], grads[1]
    return (up_grad(first[:FEAT]), down_grad(first[FEAT:]), up_grad(second[:FEAT]), down_grad(second[FEAT:]))


def solution(mesh):
    return jax.shard_map(
        per_device,
        mesh=mesh,
        in_specs=(P("mon", None),) * 4 + (P("section", "mon", None, None),) * 4,
        out_specs=(P("section", "mon", None, None),) * 4,
        check_vma=False,
    )
```

```python
import functools
import math

import jax
import jax.numpy as jnp
from jax import lax
from jax.experimental import pallas as pl
from jax.experimental.pallas import tpu as pltpu
from jax.sharding import PartitionSpec as P

MESH = pl.DeviceIdType.MESH
F32, BF16 = jnp.float32, jnp.bfloat16

ITEMS = 8
TOK = 8
FEAT = 64
HOP = 3
LANES = 128
ROWS = ITEMS * TOK


def chain_kernel(
    sections, mons, scale,
    w_own, one_in, two_in, cone_in, ctwo_in, grad_ref,
    wbuf, one, two, cone, ctwo, slope, masked_g, masked_d, send, recv, bun, xc, gbun, gxc, items,
    own_sem, own_send_sem, own_recv_sem, ring_sem, ring_send_sem, part_sem, part_send_sem,
    send_sem, recv_sem, bun_sem, xc_sem, gbun_sem, gxc_sem,
):
    sec = lax.axis_index("section")
    me = lax.axis_index("mon")
    width = mons * LANES
    chunk = 2 * LANES
    chunks = width // chunk

    barrier = pltpu.get_barrier_semaphore()
    for k in range(1, mons):
        pl.semaphore_signal(barrier, inc=1, device_id={"mon": (me + k) % mons}, device_id_type=MESH)
    for k in range(1, sections):
        pl.semaphore_signal(barrier, inc=1, device_id={"section": (sec + k) % sections}, device_id_type=MESH)

    one[...] = one_in[...]
    two[...] = two_in[...]
    cone[...] = cone_in[...]
    ctwo[...] = ctwo_in[...]
    pl.semaphore_wait(barrier, mons + sections - 2)

    chips = sections // 2
    z, core = sec // 2, sec % 2
    up = core == 1
    partner = z * 2 + 1 - core
    following = lax.rem(z + jnp.where(up, 1, chips - 1), chips) * 2 + core
    rank = chips - 1 - z

    last = lax.rem(rank + jnp.where(up, chips - 1, 1), chips)

    own_step = sections - 1 - sec
    own_copy = pltpu.make_async_copy(w_own, wbuf.at[own_step], own_sem)
    own_copy.start()
    own_push = pltpu.make_async_remote_copy(
        src_ref=w_own, dst_ref=wbuf.at[own_step], send_sem=own_send_sem, recv_sem=own_recv_sem,
        device_id={"section": partner}, device_id_type=MESH,
    )
    own_push.start()
    own_copy.wait()
    own_push.wait_recv()

    def event(at, low, high):
        place = jnp.clip(at, 0, 16 * chips - 1)
        pair = place // 16
        valid = (at == place) & (pair >= low) & (pair <= high)
        step, piece = place // 8, place % 8
        foreign = valid & (pair != rank)
        onward = valid & (pair != last)
        rows = pl.ds(pl.multiple_of(core * 32 + (piece % 2) * 16, 16), 16)
        here = wbuf.at[step, piece // 2, rows]
        return place, step, piece, here, foreign, onward

    def relay(slot):
        for at, low, high in (
            (slot - HOP * jnp.where(up, chips - rank, rank), 0, jnp.where(up, rank - 1, rank)),
            (slot - HOP * jnp.where(up, -rank, rank + chips), jnp.where(up, rank, rank + 1), chips - 1),
        ):
            place, step, piece, here, foreign, onward = event(at, low, high)

            @pl.when(foreign)
            def _():
                pltpu.make_async_copy(here, here, ring_sem.at[place]).wait()
                pltpu.make_async_remote_copy(
                    src_ref=here, dst_ref=here,
                    send_sem=part_send_sem, recv_sem=part_sem.at[step * 2 + piece // 4],
                    device_id={"section": partner}, device_id_type=MESH,
                ).start()

            if chips > 1:
                @pl.when(onward)
                def _():
                    pltpu.make_async_remote_copy(
                        src_ref=here, dst_ref=here,
                        send_sem=ring_send_sem, recv_sem=ring_sem.at[place],
                        device_id={"section": following}, device_id_type=MESH,
                    ).start()
        return 0

    ahead = HOP * (chips - 1) + 6

    def start_up(slot, carry):
        relay(slot)
        return carry

    lax.fori_loop(0, ahead, start_up, 0)

    lane = lax.broadcasted_iota(jnp.int32, (TOK, chunk), 1) % LANES
    of_block = lane // 16
    of_group = (lane // 2) % 8

    def diagonal(full, which):
        picked = full[0:TOK]
        for k in range(1, ITEMS):
            picked = jnp.where(which == k, full[k * TOK:(k + 1) * TOK], picked)
        return picked

    def spread(values, which):
        return jnp.concatenate(
            [jnp.where(which == k, values, 0.0) for k in range(ITEMS)], axis=0
        ).astype(BF16)

    def push(at, half):
        layer = sections - 1 - at // 2

        @pl.when(sec == layer)
        def _():
            pltpu.make_async_copy(bun.at[at], gbun.at[half, sec], bun_sem).start()
            pltpu.make_async_copy(xc.at[at], gxc.at[half, sec], xc_sem).start()

        @pl.when(sec != layer)
        def _():
            pltpu.make_async_remote_copy(
                src_ref=bun.at[at], dst_ref=gbun.at[half, sec],
                send_sem=bun_sem, recv_sem=gbun_sem.at[half],
                device_id={"section": layer}, device_id_type=MESH,
            ).start()
            pltpu.make_async_remote_copy(
                src_ref=xc.at[at], dst_ref=gxc.at[half, sec],
                send_sem=xc_sem, recv_sem=gxc_sem.at[half],
                device_id={"section": layer}, device_id_type=MESH,
            ).start()

    def half_step(step, half, first, w_up, w_down, source, target, cot, carry):
        at = step * 2 + half

        @pl.when(step // 2 != rank)
        def _():
            part = wbuf.at[step, pl.ds(2 * half, 2), pl.ds(0, 32)]
            pltpu.make_async_copy(part, part, part_sem.at[step * 2 + half]).wait()

        feed = source[...].astype(BF16)
        cot_bf = cot[...].astype(BF16)

        @pl.when(step > 0)
        def _():
            pltpu.make_async_copy(send.at[half, pl.ds(0, mons - 1)], send.at[half, pl.ds(0, mons - 1)], send_sem.at[half]).wait()

        for n in range(chunks):
            cols = pl.ds(n * chunk, chunk)
            pre = diagonal(jnp.dot(feed, wbuf[step, w_up, :, cols], preferred_element_type=F32), of_block)
            back = diagonal(jnp.dot(cot_bf, wbuf[step, w_down, :, cols], preferred_element_type=F32), of_group)
            sig = 1.0 / (1.0 + jnp.exp(-pre))
            slope[:, cols] = sig * (1.0 + pre * (1.0 - sig))
            tile = jnp.concatenate([pre * sig, back], axis=0).astype(BF16)
            send[half, 2 * n] = tile[:, 0:LANES]
            send[half, 2 * n + 1] = tile[:, LANES:chunk]

        for k in range(1, mons):
            peer = (me + k) % mons
            pltpu.make_async_remote_copy(
                src_ref=send.at[half, peer], dst_ref=recv.at[half, me],
                send_sem=send_sem.at[half], recv_sem=recv_sem.at[half],
                device_id={"mon": peer}, device_id_type=MESH,
            ).start()
        recv[half, me] = send[half, me]
        if first is not None:
            lax.fori_loop(0, 4, lambda k, carry: relay(first + k), 0)
        xc[at, :, 0:FEAT] = feed
        xc[at, :, FEAT:LANES] = cot_bf
        pltpu.make_async_copy(recv.at[half, pl.ds(0, mons - 1)], recv.at[half, pl.ds(0, mons - 1)], recv_sem.at[half]).wait()

        for n in range(chunks):
            cols = pl.ds(n * chunk, chunk)
            arrived = jnp.concatenate([recv[half, 2 * n], recv[half, 2 * n + 1]], axis=1).astype(F32)
            grouped = arrived[0:TOK]
            dpre = arrived[TOK:2 * TOK] * slope[:, cols]
            masked_g[:, cols] = spread(grouped, of_group)
            masked_d[:, cols] = spread(dpre, of_block)
            bun[at, :, cols] = jnp.concatenate([grouped, dpre], axis=0).astype(BF16)
            if first is not None and n in (2, 4, 6):
                relay(first + 3 + n // 2)
        trans = (((1,), (1,)), ((), ()))
        target[...] -= lax.dot_general(masked_g[...], wbuf[step, w_down], trans, preferred_element_type=F32)
        carry[...] += lax.dot_general(masked_d[...], wbuf[step, w_up], trans, preferred_element_type=F32)

        if first is None:
            push(at - sections, half)
            push(at, half)

        if first is not None:
            lax.fori_loop(7, 9, lambda k, carry: relay(first + k), 0)

    def layer_step(step, relaying):
        for half in range(2):
            first = ahead + 9 * (step * 2 + half) if relaying else None
            if half == 0:
                half_step(step, 0, first, 0, 1, one, two, ctwo, cone)
            else:
                half_step(step, 1, first, 2, 3, two, one, cone, ctwo)

    def early(step, carry):
        layer_step(step, True)
        return carry

    def late(step, carry):
        layer_step(step, False)
        return carry

    lax.fori_loop(0, sections // 2, early, 0)
    lax.fori_loop(sections // 2, sections, late, 0)

    own_push.wait_send()
    pltpu.make_async_copy(bun, bun, bun_sem).wait()
    pltpu.make_async_copy(xc, xc, xc_sem).wait()
    if chips > 1:
        sent = wbuf.at[pl.ds(0, chips - 1)]
        pltpu.make_async_copy(sent, sent, ring_send_sem).wait()
        pltpu.make_async_copy(sent, sent, part_send_sem).wait()

    for half in range(2):
        pltpu.make_async_copy(send.at[half, pl.ds(0, mons - 1)], send.at[half, pl.ds(0, mons - 1)], send_sem.at[half]).wait()
        if sections > 1:
            part = pl.ds(0, sections - 1)
            pltpu.make_async_copy(gbun.at[half, part], gbun.at[half, part], gbun_sem.at[half]).wait()
            pltpu.make_async_copy(gxc.at[half, part], gxc.at[half, part], gxc_sem.at[half]).wait()

    left = lax.broadcasted_iota(jnp.int32, (TOK, LANES), 1) < FEAT
    row = lax.broadcasted_iota(jnp.int32, (LANES, chunk), 0)
    lane2 = lax.broadcasted_iota(jnp.int32, (LANES, chunk), 1) % LANES
    which = jnp.where(row < FEAT, lane2 // 16, (lane2 // 2) % 8)
    depth = sections * 2 * TOK
    for half in range(2):
        for s in range(sections):
            block = gxc[half, s].astype(F32)
            for k in range(ITEMS):
                piece = block[k * TOK:(k + 1) * TOK]
                items[k, s * 16:s * 16 + TOK, :] = jnp.where(left, 0.0, piece)
                items[k, s * 16 + TOK:s * 16 + 16, :] = jnp.where(left, piece, 0.0)

        def grad_chunk(n, carry):
            cols = pl.ds(pl.multiple_of(n * chunk, chunk), chunk)
            rhs = gbun[half, :, :, cols].reshape(depth, chunk)
            total = None
            for k in range(ITEMS):
                one_item = lax.dot_general(
                    items[k].astype(BF16), rhs, (((0,), (0,)), ((), ())), preferred_element_type=F32
                )
                total = one_item if total is None else jnp.where(which == k, one_item, total)
            grad_ref[half, :, cols] = total * scale
            return carry

        lax.fori_loop(0, chunks, grad_chunk, 0)


def tile_up(w):
    mons = w.shape[2] // 16
    return w.reshape(ITEMS, FEAT, mons, 16).transpose(1, 2, 0, 3).reshape(FEAT, mons * LANES)


def tile_down(w):
    mons = w.shape[1] // 16
    return w.reshape(ITEMS, 2, mons, 8, FEAT).transpose(4, 2, 3, 0, 1).reshape(FEAT, mons * LANES)


def per_device(
    stream_one, stream_two, cotan_one, cotan_two, first_up, first_down, second_up, second_down
):
    sections = lax.axis_size("section")
    mons = lax.axis_size("mon")
    sec = lax.axis_index("section")
    width = mons * LANES
    tokens = stream_one.shape[1]
    w_own = jnp.stack(
        [tile_up(second_up[0]), tile_down(second_down[0]), tile_up(first_up[0]), tile_down(first_down[0])]
    )

    def mine(x):
        part = lax.dynamic_slice_in_dim(x, sec * TOK, TOK, 1)
        return part.reshape(ITEMS, FEAT, TOK).transpose(0, 2, 1).reshape(ROWS, FEAT)

    vmem = pl.BlockSpec(memory_space=pltpu.VMEM)
    grads = pl.pallas_call(
        functools.partial(chain_kernel, sections, mons, 1.0 / math.sqrt(tokens)),
        out_shape=jax.ShapeDtypeStruct((2, LANES, width), F32),
        in_specs=[pl.BlockSpec(memory_space=pl.ANY), vmem, vmem, vmem, vmem],
        out_specs=vmem,
        scratch_shapes=[
            pltpu.VMEM((sections, 4, FEAT, width), BF16),
            pltpu.VMEM((ROWS, FEAT), F32),
            pltpu.VMEM((ROWS, FEAT), F32),
            pltpu.VMEM((ROWS, FEAT), F32),
            pltpu.VMEM((ROWS, FEAT), F32),
            pltpu.VMEM((TOK, width), F32),
            pltpu.VMEM((ROWS, width), BF16),
            pltpu.VMEM((ROWS, width), BF16),
            pltpu.VMEM((2, mons, 2 * TOK, LANES), BF16),
            pltpu.VMEM((2, mons, 2 * TOK, LANES), BF16),
            pltpu.VMEM((2 * sections, 2 * TOK, width), BF16),
            pltpu.VMEM((2 * sections, ROWS, LANES), BF16),
            pltpu.VMEM((2, sections, 2 * TOK, width), BF16),
            pltpu.VMEM((2, sections, ROWS, LANES), BF16),
            pltpu.VMEM((ITEMS, sections * 2 * TOK, LANES), F32),
            pltpu.SemaphoreType.DMA,
            pltpu.SemaphoreType.DMA,
            pltpu.SemaphoreType.DMA,
            pltpu.SemaphoreType.DMA((sections * 8,)),
            pltpu.SemaphoreType.DMA,
            pltpu.SemaphoreType.DMA((sections * 2,)),
            pltpu.SemaphoreType.DMA,
            pltpu.SemaphoreType.DMA((2,)),
            pltpu.SemaphoreType.DMA((2,)),
            pltpu.SemaphoreType.DMA,
            pltpu.SemaphoreType.DMA,
            pltpu.SemaphoreType.DMA((2,)),
            pltpu.SemaphoreType.DMA((2,)),
        ],
        compiler_params=pltpu.CompilerParams(
            collective_id=0, has_side_effects=True, vmem_limit_bytes=50 * 1024 * 1024
        ),
    )(w_own, mine(stream_one), mine(stream_two), mine(cotan_one), mine(cotan_two))

    def up_grad(tiles):
        return tiles.reshape(FEAT, mons, ITEMS, 16).transpose(2, 0, 1, 3).reshape(1, ITEMS, FEAT, mons * 16)

    def down_grad(tiles):
        return tiles.reshape(FEAT, mons, 8, ITEMS, 2).transpose(3, 4, 1, 2, 0).reshape(1, ITEMS, mons * 16, FEAT)

    second, first = grads[0], grads[1]
    return (up_grad(first[:FEAT]), down_grad(first[FEAT:]), up_grad(second[:FEAT]), down_grad(second[FEAT:]))


def solution(mesh):
    return jax.shard_map(
        per_device,
        mesh=mesh,
        in_specs=(P("mon", None),) * 4 + (P("section", "mon", None, None),) * 4,
        out_specs=(P("section", "mon", None, None),) * 4,
        check_vma=False,
    )
```

```python
import functools
import math

import jax
import jax.numpy as jnp
from jax import lax
from jax.experimental import pallas as pl
from jax.experimental.pallas import tpu as pltpu
from jax.sharding import PartitionSpec as P

MESH = pl.DeviceIdType.MESH
F32, BF16 = jnp.float32, jnp.bfloat16

ITEMS = 8
TOK = 8
FEAT = 64
HOP = 6
LANES = 128
ROWS = ITEMS * TOK


def chain_kernel(
    sections, mons, scale,
    w_own, one_in, two_in, cone_in, ctwo_in, grad_ref,
    wbuf, one, two, cone, ctwo, slope, masked_g, masked_d, send, recv, bun, xc, gbun, gxc, items,
    own_sem, own_send_sem, own_recv_sem, ring_sem, ring_send_sem, part_sem, part_send_sem,
    send_sem, recv_sem, bun_sem, xc_sem, gbun_sem, gxc_sem,
):
    sec = lax.axis_index("section")
    me = lax.axis_index("mon")
    width = mons * LANES
    chunk = 2 * LANES
    chunks = width // chunk

    barrier = pltpu.get_barrier_semaphore()
    for k in range(1, mons):
        pl.semaphore_signal(barrier, inc=1, device_id={"mon": (me + k) % mons}, device_id_type=MESH)
    for k in range(1, sections):
        pl.semaphore_signal(barrier, inc=1, device_id={"section": (sec + k) % sections}, device_id_type=MESH)

    one[...] = one_in[...]
    two[...] = two_in[...]
    cone[...] = cone_in[...]
    ctwo[...] = ctwo_in[...]
    pl.semaphore_wait(barrier, mons + sections - 2)

    chips = sections // 2
    z, core = sec // 2, sec % 2
    up = core == 1
    partner = z * 2 + 1 - core
    following = lax.rem(z + jnp.where(up, 1, chips - 1), chips) * 2 + core
    rank = chips - 1 - z

    last = lax.rem(rank + jnp.where(up, chips - 1, 1), chips)

    own_step = sections - 1 - sec
    own_copy = pltpu.make_async_copy(w_own, wbuf.at[own_step], own_sem)
    own_copy.start()
    own_push = pltpu.make_async_remote_copy(
        src_ref=w_own, dst_ref=wbuf.at[own_step], send_sem=own_send_sem, recv_sem=own_recv_sem,
        device_id={"section": partner}, device_id_type=MESH,
    )
    own_push.start()
    own_copy.wait()
    own_push.wait_recv()

    def event(at, low, high):
        place = jnp.clip(at, 0, 16 * chips - 1)
        pair = place // 16
        valid = (at == place) & (pair >= low) & (pair <= high)
        step, piece = place // 8, place % 8
        foreign = valid & (pair != rank)
        onward = valid & (pair != last)
        rows = pl.ds(pl.multiple_of(core * 32 + (piece % 2) * 16, 16), 16)
        here = wbuf.at[step, piece // 2, rows]
        return place, step, piece, here, foreign, onward

    def relay(slot):
        for at, low, high in (
            (slot - HOP * jnp.where(up, chips - rank, rank), 0, jnp.where(up, rank - 1, rank)),
            (slot - HOP * jnp.where(up, -rank, rank + chips), jnp.where(up, rank, rank + 1), chips - 1),
        ):
            place, step, piece, here, foreign, onward = event(at, low, high)

            @pl.when(foreign)
            def _():
                pltpu.make_async_copy(here, here, ring_sem.at[place]).wait()
                pltpu.make_async_remote_copy(
                    src_ref=here, dst_ref=here,
                    send_sem=part_send_sem, recv_sem=part_sem.at[step * 2 + piece // 4],
                    device_id={"section": partner}, device_id_type=MESH,
                ).start()

            if chips > 1:
                @pl.when(onward)
                def _():
                    pltpu.make_async_remote_copy(
                        src_ref=here, dst_ref=here,
                        send_sem=ring_send_sem, recv_sem=ring_sem.at[place],
                        device_id={"section": following}, device_id_type=MESH,
                    ).start()
        return 0

    ahead = HOP * (chips - 1) + 6

    def start_up(slot, carry):
        relay(slot)
        return carry

    lax.fori_loop(0, ahead, start_up, 0)

    lane = lax.broadcasted_iota(jnp.int32, (TOK, chunk), 1) % LANES
    of_block = lane // 16
    of_group = (lane // 2) % 8

    def diagonal(full, which):
        picked = full[0:TOK]
        for k in range(1, ITEMS):
            picked = jnp.where(which == k, full[k * TOK:(k + 1) * TOK], picked)
        return picked

    def spread(values, which):
        return jnp.concatenate(
            [jnp.where(which == k, values, 0.0) for k in range(ITEMS)], axis=0
        ).astype(BF16)

    def push(at, half):
        layer = sections - 1 - at // 2

        @pl.when(sec == layer)
        def _():
            pltpu.make_async_copy(bun.at[at], gbun.at[half, sec], bun_sem).start()
            pltpu.make_async_copy(xc.at[at], gxc.at[half, sec], xc_sem).start()

        @pl.when(sec != layer)
        def _():
            pltpu.make_async_remote_copy(
                src_ref=bun.at[at], dst_ref=gbun.at[half, sec],
                send_sem=bun_sem, recv_sem=gbun_sem.at[half],
                device_id={"section": layer}, device_id_type=MESH,
            ).start()
            pltpu.make_async_remote_copy(
                src_ref=xc.at[at], dst_ref=gxc.at[half, sec],
                send_sem=xc_sem, recv_sem=gxc_sem.at[half],
                device_id={"section": layer}, device_id_type=MESH,
            ).start()

    def half_step(step, half, first, w_up, w_down, source, target, cot, carry):
        at = step * 2 + half

        @pl.when(step // 2 != rank)
        def _():
            part = wbuf.at[step, pl.ds(2 * half, 2), pl.ds(0, 32)]
            pltpu.make_async_copy(part, part, part_sem.at[step * 2 + half]).wait()

        feed = source[...].astype(BF16)
        cot_bf = cot[...].astype(BF16)

        @pl.when(step > 0)
        def _():
            pltpu.make_async_copy(send.at[half, pl.ds(0, mons - 1)], send.at[half, pl.ds(0, mons - 1)], send_sem.at[half]).wait()

        for n in range(chunks):
            cols = pl.ds(n * chunk, chunk)
            pre = diagonal(jnp.dot(feed, wbuf[step, w_up, :, cols], preferred_element_type=F32), of_block)
            back = diagonal(jnp.dot(cot_bf, wbuf[step, w_down, :, cols], preferred_element_type=F32), of_group)
            sig = 1.0 / (1.0 + jnp.exp(-pre))
            slope[:, cols] = sig * (1.0 + pre * (1.0 - sig))
            tile = jnp.concatenate([pre * sig, back], axis=0).astype(BF16)
            send[half, 2 * n] = tile[:, 0:LANES]
            send[half, 2 * n + 1] = tile[:, LANES:chunk]

        for k in range(1, mons):
            peer = (me + k) % mons
            pltpu.make_async_remote_copy(
                src_ref=send.at[half, peer], dst_ref=recv.at[half, me],
                send_sem=send_sem.at[half], recv_sem=recv_sem.at[half],
                device_id={"mon": peer}, device_id_type=MESH,
            ).start()
        recv[half, me] = send[half, me]
        if first is not None:
            lax.fori_loop(0, 10, lambda k, carry: relay(first + k), 0)
        xc[at, :, 0:FEAT] = feed
        xc[at, :, FEAT:LANES] = cot_bf
        pltpu.make_async_copy(recv.at[half, pl.ds(0, mons - 1)], recv.at[half, pl.ds(0, mons - 1)], recv_sem.at[half]).wait()

        for n in range(chunks):
            cols = pl.ds(n * chunk, chunk)
            arrived = jnp.concatenate([recv[half, 2 * n], recv[half, 2 * n + 1]], axis=1).astype(F32)
            grouped = arrived[0:TOK]
            dpre = arrived[TOK:2 * TOK] * slope[:, cols]
            masked_g[:, cols] = spread(grouped, of_group)
            masked_d[:, cols] = spread(dpre, of_block)
            bun[at, :, cols] = jnp.concatenate([grouped, dpre], axis=0).astype(BF16)
        trans = (((1,), (1,)), ((), ()))
        target[...] -= lax.dot_general(masked_g[...], wbuf[step, w_down], trans, preferred_element_type=F32)
        carry[...] += lax.dot_general(masked_d[...], wbuf[step, w_up], trans, preferred_element_type=F32)

        @pl.when(step >= sections // 2)
        def _():
            push(at - sections, half)
            push(at, half)


    def layer_step(step, relaying):
        for half in range(2):
            first = ahead + 10 * (step * 2 + half) if relaying else None
            if half == 0:
                half_step(step, 0, first, 0, 1, one, two, ctwo, cone)
            else:
                half_step(step, 1, first, 2, 3, two, one, cone, ctwo)

    def early(step, carry):
        layer_step(step, True)
        return carry

    lax.fori_loop(0, sections, early, 0)

    own_push.wait_send()
    pltpu.make_async_copy(bun, bun, bun_sem).wait()
    pltpu.make_async_copy(xc, xc, xc_sem).wait()
    if chips > 1:
        sent = wbuf.at[pl.ds(0, chips - 1)]
        pltpu.make_async_copy(sent, sent, ring_send_sem).wait()
        pltpu.make_async_copy(sent, sent, part_send_sem).wait()

    for half in range(2):
        pltpu.make_async_copy(send.at[half, pl.ds(0, mons - 1)], send.at[half, pl.ds(0, mons - 1)], send_sem.at[half]).wait()
        if sections > 1:
            part = pl.ds(0, sections - 1)
            pltpu.make_async_copy(gbun.at[half, part], gbun.at[half, part], gbun_sem.at[half]).wait()
            pltpu.make_async_copy(gxc.at[half, part], gxc.at[half, part], gxc_sem.at[half]).wait()

    left = lax.broadcasted_iota(jnp.int32, (TOK, LANES), 1) < FEAT
    row = lax.broadcasted_iota(jnp.int32, (LANES, chunk), 0)
    lane2 = lax.broadcasted_iota(jnp.int32, (LANES, chunk), 1) % LANES
    which = jnp.where(row < FEAT, lane2 // 16, (lane2 // 2) % 8)
    depth = sections * 2 * TOK
    for half in range(2):
        for s in range(sections):
            block = gxc[half, s].astype(F32)
            for k in range(ITEMS):
                piece = block[k * TOK:(k + 1) * TOK]
                items[k, s * 16:s * 16 + TOK, :] = jnp.where(left, 0.0, piece)
                items[k, s * 16 + TOK:s * 16 + 16, :] = jnp.where(left, piece, 0.0)

        def grad_chunk(n, carry):
            cols = pl.ds(pl.multiple_of(n * chunk, chunk), chunk)
            rhs = gbun[half, :, :, cols].reshape(depth, chunk)
            total = None
            for k in range(ITEMS):
                one_item = lax.dot_general(
                    items[k].astype(BF16), rhs, (((0,), (0,)), ((), ())), preferred_element_type=F32
                )
                total = one_item if total is None else jnp.where(which == k, one_item, total)
            grad_ref[half, :, cols] = total * scale
            return carry

        lax.fori_loop(0, chunks, grad_chunk, 0)


def tile_up(w):
    mons = w.shape[2] // 16
    return w.reshape(ITEMS, FEAT, mons, 16).transpose(1, 2, 0, 3).reshape(FEAT, mons * LANES)


def tile_down(w):
    mons = w.shape[1] // 16
    return w.reshape(ITEMS, 2, mons, 8, FEAT).transpose(4, 2, 3, 0, 1).reshape(FEAT, mons * LANES)


def per_device(
    stream_one, stream_two, cotan_one, cotan_two, first_up, first_down, second_up, second_down
):
    sections = lax.axis_size("section")
    mons = lax.axis_size("mon")
    sec = lax.axis_index("section")
    width = mons * LANES
    tokens = stream_one.shape[1]
    w_own = jnp.stack(
        [tile_up(second_up[0]), tile_down(second_down[0]), tile_up(first_up[0]), tile_down(first_down[0])]
    )

    def mine(x):
        part = lax.dynamic_slice_in_dim(x, sec * TOK, TOK, 1)
        return part.reshape(ITEMS, FEAT, TOK).transpose(0, 2, 1).reshape(ROWS, FEAT)

    vmem = pl.BlockSpec(memory_space=pltpu.VMEM)
    grads = pl.pallas_call(
        functools.partial(chain_kernel, sections, mons, 1.0 / math.sqrt(tokens)),
        out_shape=jax.ShapeDtypeStruct((2, LANES, width), F32),
        in_specs=[pl.BlockSpec(memory_space=pl.ANY), vmem, vmem, vmem, vmem],
        out_specs=vmem,
        scratch_shapes=[
            pltpu.VMEM((sections, 4, FEAT, width), BF16),
            pltpu.VMEM((ROWS, FEAT), F32),
            pltpu.VMEM((ROWS, FEAT), F32),
            pltpu.VMEM((ROWS, FEAT), F32),
            pltpu.VMEM((ROWS, FEAT), F32),
            pltpu.VMEM((TOK, width), F32),
            pltpu.VMEM((ROWS, width), BF16),
            pltpu.VMEM((ROWS, width), BF16),
            pltpu.VMEM((2, mons, 2 * TOK, LANES), BF16),
            pltpu.VMEM((2, mons, 2 * TOK, LANES), BF16),
            pltpu.VMEM((2 * sections, 2 * TOK, width), BF16),
            pltpu.VMEM((2 * sections, ROWS, LANES), BF16),
            pltpu.VMEM((2, sections, 2 * TOK, width), BF16),
            pltpu.VMEM((2, sections, ROWS, LANES), BF16),
            pltpu.VMEM((ITEMS, sections * 2 * TOK, LANES), F32),
            pltpu.SemaphoreType.DMA,
            pltpu.SemaphoreType.DMA,
            pltpu.SemaphoreType.DMA,
            pltpu.SemaphoreType.DMA((sections * 8,)),
            pltpu.SemaphoreType.DMA,
            pltpu.SemaphoreType.DMA((sections * 2,)),
            pltpu.SemaphoreType.DMA,
            pltpu.SemaphoreType.DMA((2,)),
            pltpu.SemaphoreType.DMA((2,)),
            pltpu.SemaphoreType.DMA,
            pltpu.SemaphoreType.DMA,
            pltpu.SemaphoreType.DMA((2,)),
            pltpu.SemaphoreType.DMA((2,)),
        ],
        compiler_params=pltpu.CompilerParams(
            collective_id=0, has_side_effects=True, vmem_limit_bytes=50 * 1024 * 1024
        ),
    )(w_own, mine(stream_one), mine(stream_two), mine(cotan_one), mine(cotan_two))

    def up_grad(tiles):
        return tiles.reshape(FEAT, mons, ITEMS, 16).transpose(2, 0, 1, 3).reshape(1, ITEMS, FEAT, mons * 16)

    def down_grad(tiles):
        return tiles.reshape(FEAT, mons, 8, ITEMS, 2).transpose(3, 4, 1, 2, 0).reshape(1, ITEMS, mons * 16, FEAT)

    second, first = grads[0], grads[1]
    return (up_grad(first[:FEAT]), down_grad(first[FEAT:]), up_grad(second[:FEAT]), down_grad(second[FEAT:]))


def solution(mesh):
    return jax.shard_map(
        per_device,
        mesh=mesh,
        in_specs=(P("mon", None),) * 4 + (P("section", "mon", None, None),) * 4,
        out_specs=(P("section", "mon", None, None),) * 4,
        check_vma=False,
    )
```

```python
import functools
import math

import jax
import jax.numpy as jnp
from jax import lax
from jax.experimental import pallas as pl
from jax.experimental.pallas import tpu as pltpu
from jax.sharding import PartitionSpec as P

MESH = pl.DeviceIdType.MESH
F32, BF16 = jnp.float32, jnp.bfloat16

ITEMS = 8
TOK = 8
FEAT = 64
HOP = 5
LANES = 128
ROWS = ITEMS * TOK


def chain_kernel(
    sections, mons, scale,
    w_own, one_in, two_in, cone_in, ctwo_in, grad_ref,
    wbuf, one, two, cone, ctwo, slope, masked_g, masked_d, send, recv, bun, xc, gbun, gxc, items,
    own_sem, own_send_sem, own_recv_sem, ring_sem, ring_send_sem, part_sem, part_send_sem,
    send_sem, recv_sem, bun_sem, xc_sem, gbun_sem, gxc_sem,
):
    sec = lax.axis_index("section")
    me = lax.axis_index("mon")
    width = mons * LANES
    side = math.isqrt(mons)
    offsets = [(dx, dy) for dx in range(side) for dy in range(side) if dx or dy]
    offsets.sort(key=lambda o: -sum(min(d, side - d) for d in o))
    chunk = 2 * LANES
    chunks = width // chunk

    barrier = pltpu.get_barrier_semaphore()
    for k in range(1, mons):
        pl.semaphore_signal(barrier, inc=1, device_id={"mon": (me + k) % mons}, device_id_type=MESH)
    for k in range(1, sections):
        pl.semaphore_signal(barrier, inc=1, device_id={"section": (sec + k) % sections}, device_id_type=MESH)

    one[...] = one_in[...]
    two[...] = two_in[...]
    cone[...] = cone_in[...]
    ctwo[...] = ctwo_in[...]
    pl.semaphore_wait(barrier, mons + sections - 2)

    chips = sections // 2
    z, core = sec // 2, sec % 2
    up = core == 1
    partner = z * 2 + 1 - core
    following = lax.rem(z + jnp.where(up, 1, chips - 1), chips) * 2 + core
    rank = chips - 1 - z

    last = lax.rem(rank + jnp.where(up, chips - 1, 1), chips)

    own_step = sections - 1 - sec
    own_copy = pltpu.make_async_copy(w_own, wbuf.at[own_step], own_sem)
    own_copy.start()
    own_push = pltpu.make_async_remote_copy(
        src_ref=w_own, dst_ref=wbuf.at[own_step], send_sem=own_send_sem, recv_sem=own_recv_sem,
        device_id={"section": partner}, device_id_type=MESH,
    )
    own_push.start()
    own_copy.wait()
    own_push.wait_recv()

    def event(at, low, high):
        place = jnp.clip(at, 0, 16 * chips - 1)
        pair = place // 16
        valid = (at == place) & (pair >= low) & (pair <= high)
        step, piece = place // 8, place % 8
        foreign = valid & (pair != rank)
        onward = valid & (pair != last)
        rows = pl.ds(pl.multiple_of(core * 32 + (piece % 2) * 16, 16), 16)
        here = wbuf.at[step, piece // 2, rows]
        return place, step, piece, here, foreign, onward

    def relay(slot):
        for at, low, high in (
            (slot - HOP * jnp.where(up, chips - rank, rank), 0, jnp.where(up, rank - 1, rank)),
            (slot - HOP * jnp.where(up, -rank, rank + chips), jnp.where(up, rank, rank + 1), chips - 1),
        ):
            place, step, piece, here, foreign, onward = event(at, low, high)

            @pl.when(foreign)
            def _():
                pltpu.make_async_copy(here, here, ring_sem.at[place]).wait()
                pltpu.make_async_remote_copy(
                    src_ref=here, dst_ref=here,
                    send_sem=part_send_sem, recv_sem=part_sem.at[step * 2 + piece // 4],
                    device_id={"section": partner}, device_id_type=MESH,
                ).start()

            if chips > 1:
                @pl.when(onward)
                def _():
                    pltpu.make_async_remote_copy(
                        src_ref=here, dst_ref=here,
                        send_sem=ring_send_sem, recv_sem=ring_sem.at[place],
                        device_id={"section": following}, device_id_type=MESH,
                    ).start()
        return 0

    ahead = HOP * (chips - 1) + 6

    def start_up(slot, carry):
        relay(slot)
        return carry

    lax.fori_loop(0, ahead, start_up, 0)

    lane = lax.broadcasted_iota(jnp.int32, (TOK, chunk), 1) % LANES
    of_block = lane // 16
    of_group = (lane // 2) % 8

    def diagonal(full, which):
        picked = full[0:TOK]
        for k in range(1, ITEMS):
            picked = jnp.where(which == k, full[k * TOK:(k + 1) * TOK], picked)
        return picked

    def spread(values, which):
        return jnp.concatenate(
            [jnp.where(which == k, values, 0.0) for k in range(ITEMS)], axis=0
        ).astype(BF16)

    def push(at, half):
        layer = sections - 1 - at // 2

        @pl.when(sec == layer)
        def _():
            pltpu.make_async_copy(bun.at[at], gbun.at[half, sec], gbun_sem.at[half]).start()
            pltpu.make_async_copy(xc.at[at], gxc.at[half, sec], gxc_sem.at[half]).start()

        @pl.when(sec != layer)
        def _():
            pltpu.make_async_remote_copy(
                src_ref=bun.at[at], dst_ref=gbun.at[half, sec],
                send_sem=bun_sem, recv_sem=gbun_sem.at[half],
                device_id={"section": layer}, device_id_type=MESH,
            ).start()
            pltpu.make_async_remote_copy(
                src_ref=xc.at[at], dst_ref=gxc.at[half, sec],
                send_sem=xc_sem, recv_sem=gxc_sem.at[half],
                device_id={"section": layer}, device_id_type=MESH,
            ).start()

    def half_step(step, half, first, w_up, w_down, source, target, cot, carry):
        at = step * 2 + half

        @pl.when(step // 2 != rank)
        def _():
            part = wbuf.at[step, pl.ds(2 * half, 2), pl.ds(0, 32)]
            pltpu.make_async_copy(part, part, part_sem.at[step * 2 + half]).wait()

        feed = source[...].astype(BF16)
        cot_bf = cot[...].astype(BF16)

        @pl.when(step > 0)
        def _():
            pltpu.make_async_copy(send.at[half, pl.ds(0, mons - 1)], send.at[half, pl.ds(0, mons - 1)], send_sem.at[half]).wait()

        for n in range(chunks):
            cols = pl.ds(n * chunk, chunk)
            pre = diagonal(jnp.dot(feed, wbuf[step, w_up, :, cols], preferred_element_type=F32), of_block)
            back = diagonal(jnp.dot(cot_bf, wbuf[step, w_down, :, cols], preferred_element_type=F32), of_group)
            sig = 1.0 / (1.0 + jnp.exp(-pre))
            slope[:, cols] = sig * (1.0 + pre * (1.0 - sig))
            tile = jnp.concatenate([pre * sig, back], axis=0).astype(BF16)
            send[half, 2 * n] = tile[:, 0:LANES]
            send[half, 2 * n + 1] = tile[:, LANES:chunk]

        for dx, dy in offsets:
            peer = (me // side + dx) % side * side + (me % side + dy) % side
            pltpu.make_async_remote_copy(
                src_ref=send.at[half, peer], dst_ref=recv.at[half, me],
                send_sem=send_sem.at[half], recv_sem=recv_sem.at[half],
                device_id={"mon": peer}, device_id_type=MESH,
            ).start()
        recv[half, me] = send[half, me]
        if first is not None:
            lax.fori_loop(0, 10, lambda k, carry: relay(first + k), 0)

        @pl.when(step >= sections // 2)
        def _():
            push(at - sections, half)

        @pl.when(at > sections)
        def _():
            push(at - 1, 1 - half)

        xc[at, :, 0:FEAT] = feed
        xc[at, :, FEAT:LANES] = cot_bf
        pltpu.make_async_copy(recv.at[half, pl.ds(0, mons - 1)], recv.at[half, pl.ds(0, mons - 1)], recv_sem.at[half]).wait()

        for n in range(chunks):
            cols = pl.ds(n * chunk, chunk)
            arrived = jnp.concatenate([recv[half, 2 * n], recv[half, 2 * n + 1]], axis=1).astype(F32)
            grouped = arrived[0:TOK]
            dpre = arrived[TOK:2 * TOK] * slope[:, cols]
            masked_g[:, cols] = spread(grouped, of_group)
            masked_d[:, cols] = spread(dpre, of_block)
            bun[at, :, cols] = jnp.concatenate([grouped, dpre], axis=0).astype(BF16)
        trans = (((1,), (1,)), ((), ()))
        target[...] -= lax.dot_general(masked_g[...], wbuf[step, w_down], trans, preferred_element_type=F32)
        carry[...] += lax.dot_general(masked_d[...], wbuf[step, w_up], trans, preferred_element_type=F32)

    def layer_step(step, relaying):
        for half in range(2):
            first = ahead + 10 * (step * 2 + half) if relaying else None
            if half == 0:
                half_step(step, 0, first, 0, 1, one, two, ctwo, cone)
            else:
                half_step(step, 1, first, 2, 3, two, one, cone, ctwo)

    def early(step, carry):
        layer_step(step, True)
        return carry

    def late(step, carry):
        layer_step(step, False)
        return carry

    relayed = min(sections, -(-((16 + 2 * HOP) * chips - ahead) // 20))
    lax.fori_loop(0, relayed, early, 0)
    lax.fori_loop(relayed, sections, late, 0)

    push(2 * sections - 1, 1)

    left = lax.broadcasted_iota(jnp.int32, (TOK, LANES), 1) < FEAT
    row = lax.broadcasted_iota(jnp.int32, (LANES, chunk), 0)
    lane2 = lax.broadcasted_iota(jnp.int32, (LANES, chunk), 1) % LANES
    which = jnp.where(row < FEAT, lane2 // 16, (lane2 // 2) % 8)
    depth = sections * 2 * TOK
    for half in range(2):
        pltpu.make_async_copy(gbun.at[half], gbun.at[half], gbun_sem.at[half]).wait()
        pltpu.make_async_copy(gxc.at[half], gxc.at[half], gxc_sem.at[half]).wait()
        for s in range(sections):
            block = gxc[half, s].astype(F32)
            for k in range(ITEMS):
                piece = block[k * TOK:(k + 1) * TOK]
                items[k, s * 16:s * 16 + TOK, :] = jnp.where(left, 0.0, piece)
                items[k, s * 16 + TOK:s * 16 + 16, :] = jnp.where(left, piece, 0.0)

        def grad_chunk(n, carry):
            cols = pl.ds(pl.multiple_of(n * chunk, chunk), chunk)
            rhs = gbun[half, :, :, cols].reshape(depth, chunk)
            total = None
            for k in range(ITEMS):
                one_item = lax.dot_general(
                    items[k].astype(BF16), rhs, (((0,), (0,)), ((), ())), preferred_element_type=F32
                )
                total = one_item if total is None else jnp.where(which == k, one_item, total)
            grad_ref[half, :, cols] = total * scale
            return carry

        lax.fori_loop(0, chunks, grad_chunk, 0)

    own_push.wait_send()
    for half in range(2):
        pltpu.make_async_copy(send.at[half, pl.ds(0, mons - 1)], send.at[half, pl.ds(0, mons - 1)], send_sem.at[half]).wait()
    if sections > 1:
        pushed = pl.ds(0, 2 * sections - 2)
        pltpu.make_async_copy(bun.at[pushed], bun.at[pushed], bun_sem).wait()
        pltpu.make_async_copy(xc.at[pushed], xc.at[pushed], xc_sem).wait()
    if chips > 1:
        sent = wbuf.at[pl.ds(0, chips - 1)]
        pltpu.make_async_copy(sent, sent, ring_send_sem).wait()
        pltpu.make_async_copy(sent, sent, part_send_sem).wait()


def tile_up(w):
    mons = w.shape[2] // 16
    return w.reshape(ITEMS, FEAT, mons, 16).transpose(1, 2, 0, 3).reshape(FEAT, mons * LANES)


def tile_down(w):
    mons = w.shape[1] // 16
    return w.reshape(ITEMS, 2, mons, 8, FEAT).transpose(4, 2, 3, 0, 1).reshape(FEAT, mons * LANES)


def per_device(
    stream_one, stream_two, cotan_one, cotan_two, first_up, first_down, second_up, second_down
):
    sections = lax.axis_size("section")
    mons = lax.axis_size("mon")
    sec = lax.axis_index("section")
    width = mons * LANES
    tokens = stream_one.shape[1]
    w_own = jnp.stack(
        [tile_up(second_up[0]), tile_down(second_down[0]), tile_up(first_up[0]), tile_down(first_down[0])]
    )

    def mine(x):
        part = lax.dynamic_slice_in_dim(x, sec * TOK, TOK, 1)
        return part.reshape(ITEMS, FEAT, TOK).transpose(0, 2, 1).reshape(ROWS, FEAT)

    vmem = pl.BlockSpec(memory_space=pltpu.VMEM)
    grads = pl.pallas_call(
        functools.partial(chain_kernel, sections, mons, 1.0 / math.sqrt(tokens)),
        out_shape=jax.ShapeDtypeStruct((2, LANES, width), F32),
        in_specs=[pl.BlockSpec(memory_space=pl.ANY), vmem, vmem, vmem, vmem],
        out_specs=vmem,
        scratch_shapes=[
            pltpu.VMEM((sections, 4, FEAT, width), BF16),
            pltpu.VMEM((ROWS, FEAT), F32),
            pltpu.VMEM((ROWS, FEAT), F32),
            pltpu.VMEM((ROWS, FEAT), F32),
            pltpu.VMEM((ROWS, FEAT), F32),
            pltpu.VMEM((TOK, width), F32),
            pltpu.VMEM((ROWS, width), BF16),
            pltpu.VMEM((ROWS, width), BF16),
            pltpu.VMEM((2, mons, 2 * TOK, LANES), BF16),
            pltpu.VMEM((2, mons, 2 * TOK, LANES), BF16),
            pltpu.VMEM((2 * sections, 2 * TOK, width), BF16),
            pltpu.VMEM((2 * sections, ROWS, LANES), BF16),
            pltpu.VMEM((2, sections, 2 * TOK, width), BF16),
            pltpu.VMEM((2, sections, ROWS, LANES), BF16),
            pltpu.VMEM((ITEMS, sections * 2 * TOK, LANES), F32),
            pltpu.SemaphoreType.DMA,
            pltpu.SemaphoreType.DMA,
            pltpu.SemaphoreType.DMA,
            pltpu.SemaphoreType.DMA((sections * 8,)),
            pltpu.SemaphoreType.DMA,
            pltpu.SemaphoreType.DMA((sections * 2,)),
            pltpu.SemaphoreType.DMA,
            pltpu.SemaphoreType.DMA((2,)),
            pltpu.SemaphoreType.DMA((2,)),
            pltpu.SemaphoreType.DMA,
            pltpu.SemaphoreType.DMA,
            pltpu.SemaphoreType.DMA((2,)),
            pltpu.SemaphoreType.DMA((2,)),
        ],
        compiler_params=pltpu.CompilerParams(
            collective_id=0, has_side_effects=True, vmem_limit_bytes=50 * 1024 * 1024
        ),
    )(w_own, mine(stream_one), mine(stream_two), mine(cotan_one), mine(cotan_two))

    def up_grad(tiles):
        return tiles.reshape(FEAT, mons, ITEMS, 16).transpose(2, 0, 1, 3).reshape(1, ITEMS, FEAT, mons * 16)

    def down_grad(tiles):
        return tiles.reshape(FEAT, mons, 8, ITEMS, 2).transpose(3, 4, 1, 2, 0).reshape(1, ITEMS, mons * 16, FEAT)

    second, first = grads[0], grads[1]
    return (up_grad(first[:FEAT]), down_grad(first[FEAT:]), up_grad(second[:FEAT]), down_grad(second[FEAT:]))


def solution(mesh):
    return jax.shard_map(
        per_device,
        mesh=mesh,
        in_specs=(P("mon", None),) * 4 + (P("section", "mon", None, None),) * 4,
        out_specs=(P("section", "mon", None, None),) * 4,
        check_vma=False,
    )
```
